1024 devices in a mesh: domain: 128 (over x, z_lo, core), band: 8 (over y, z_hi).
Axes of the slice: x: 4, y: 4, z: 32 (z_hi: 2, z_lo: 16; z = z_hi * 16 + z_lo), core: 2. Of those that a mesh axis runs over, the one named last changes fastest.
Arguments:
- wavefunctions: bfloat16 [49152, 16384], P('domain', 'band'), may hold values from -6 to 6
- rotation: bfloat16 [16384, 1024], P('band', 'domain'), may hold values from -0.1875 to 0.1875
- cell_matrices: bfloat16 [128, 512, 512], P('domain'), may hold values from -0.25 to 0.25
- cell_nodes: int32 [128, 512], P('domain'), may hold values from 0 to 511, as said below
- face_map: int32 [16384], P('domain'), may hold values from 0 to 383, as said below
Outputs:
- applied: float32 [49152, 1024], P('domain', 'band')
The draws below stay inside these ranges and needn't reach their ends.
Inputs may be any that keep to these rules, and one draw needn't show every extreme that they name: `cell_nodes`: each cell names 512 distinct positions of its device's extended list (the 384 own nodes, then the 128 shared nodes of the next device); consecutive cells of a device share 128 positions; only the last cell of each device names shared nodes, and it names all of them. `face_map`: each device's block holds 128 distinct own nodes, all of them nodes of its first cell that no other of its cells names.
All inputs are finite; a program needn't handle non-finite values.
Results may differ from the reference program's by a relative error of at most 0.0029.
Values may be sent and summed in bfloat16 or wider, within the bound.
A program may use at most 32 MiB of HBM per device.

```python
import jax
import jax.numpy as jnp
from jax import lax

STATES = 16384
OUT = 1024
CELL_NODES = 512
FACE = 128
CELL_DEV = 1
NODE_DEV = 384
NODES = 49152
CELLS = 128


def draw_cell_nodes(key, part):
    domain_count = CELLS // CELL_DEV
    stride = CELL_NODES - FACE

    def one_cell(cell_key, cell_number):
        return jax.random.permutation(cell_key, CELL_NODES) + cell_number * stride

    def one_device(device_key):
        cell_keys = jax.random.split(device_key, CELL_DEV)
        return jax.vmap(one_cell)(cell_keys, jnp.arange(CELL_DEV))
    own_key = jax.random.fold_in(key, 11)
    result = jax.vmap(one_device)(jax.random.split(own_key, domain_count))
    return result.reshape(CELLS, CELL_NODES).astype(jnp.int32)


def draw_face_map(key, part):
    domain_count = NODES // NODE_DEV
    stride = CELL_NODES - FACE

    def one_device(device_key):
        first_key, second_key = jax.random.split(device_key)
        chosen = jax.random.permutation(first_key, stride - 1)[:FACE - 1]
        with_top = jnp.concatenate([chosen, jnp.full((1,), stride - 1, chosen.dtype)])
        return jax.random.permutation(second_key, with_top)
    own_key = jax.random.fold_in(key, 23)
    result = jax.vmap(one_device)(jax.random.split(own_key, domain_count))
    return result.reshape(FACE * domain_count).astype(jnp.int32)


def with_spikes(entries, key, source, target, shards_of, factor):
    owner, partner = [(jnp.arange(entries.shape[axis_at]) // (entries.shape[axis_at] // shards_of)).reshape([-1 if axis == axis_at else 1 for axis in range(entries.ndim)]) for axis_at in (source, target)]
    chosen = jax.random.permutation(key, shards_of)[partner]
    strong = (owner == chosen) | (owner == (partner + shards_of // 2) % shards_of)
    return jnp.where(strong, factor * entries, entries)


def levels(stream_key, extent, pieces, low, top_value):
    def one(dim, shards_of):
        draws = jax.random.uniform(jax.random.fold_in(jax.random.fold_in(stream_key, 6), dim), (shards_of,), jnp.float32, low / len(pieces), top_value / len(pieces))
        return jnp.repeat(jnp.exp(draws), extent[dim] // shards_of).reshape((-1,) + (1,) * (len(extent) - dim - 1))

    loudness = one(*pieces[0])
    for cut in pieces[1:]:
        loudness = loudness * one(*cut)
    return loudness


def gaussian(stream_key, dims, scale, most, shards=(), held_as=jnp.bfloat16):
    gain = levels(stream_key, dims, shards, -0.22, 0.18) if shards else 1.0
    drawn = jax.random.normal(stream_key, dims, jnp.float32) * scale * gain
    return jnp.minimum(jnp.maximum(drawn, -most), most).astype(held_as)


def gaussian_with(key, extent, spread, limit, shards, heavy, held_as=jnp.bfloat16):
    drawn = spread * jax.random.normal(key, extent, jnp.float32)
    if shards:
        drawn = drawn * levels(key, extent, shards, -0.22, 0.18)
    return jnp.clip(with_spikes(drawn, jax.random.fold_in(key, 3), *heavy), -limit, limit).astype(held_as)


def setup_inputs(seed: int = 0) -> dict:
    streams_of = jax.random.split(jax.random.key(seed), 6)
    return {
        "wavefunctions": gaussian(streams_of[0], (NODES, STATES), 1.0, 6.0, ((0, 128), (1, 8))),
        "rotation": gaussian_with(streams_of[1], (STATES, OUT), STATES ** -0.5, 0.1875, ((0, 8), (1, 128)), (0, 1, 128, 5.5)),
        "cell_matrices": gaussian(streams_of[2], (CELLS, CELL_NODES, CELL_NODES), CELL_NODES ** -0.5, 0.25, ((0, 128),)),
        "cell_nodes": draw_cell_nodes(jax.random.fold_in(streams_of[5], 71), 0),
        "face_map": draw_face_map(jax.random.fold_in(streams_of[5], 71), 0),
    }


def reference(wavefunctions, rotation, cell_matrices, cell_nodes, face_map):
    domain_count = NODES // NODE_DEV
    rotation_wide = rotation.astype(jnp.float32)
    row_blocks = wavefunctions.reshape(domain_count, NODE_DEV, STATES)

    def rotate_block(block):
        return jnp.dot(block.astype(jnp.float32), rotation_wide, precision=lax.Precision.HIGHEST).astype(jnp.bfloat16)

    blocks = lax.map(rotate_block, row_blocks)
    maps = face_map.reshape(domain_count, FACE)
    next_blocks = jnp.concatenate([blocks[1:], jnp.zeros((1, NODE_DEV, OUT), jnp.bfloat16)], axis=0)
    next_maps = jnp.concatenate([maps[1:], jnp.zeros((1, FACE), jnp.int32)], axis=0)
    matrices = cell_matrices.reshape(domain_count, CELL_DEV, CELL_NODES, CELL_NODES)
    nodes = cell_nodes.reshape(domain_count, CELL_DEV, CELL_NODES)

    def one_domain(items):
        own, after_block, after_map, mats, index_list = items
        incoming = jnp.take(after_block, after_map, axis=0)
        extended = jnp.concatenate([own, incoming], axis=0)
        gathered = jnp.take(extended, index_list, axis=0).astype(jnp.float32)
        products = jnp.einsum("cij,cjo->cio", mats.astype(jnp.float32), gathered)
        return jax.ops.segment_sum(products.reshape(-1, OUT), index_list.reshape(-1), num_segments=NODE_DEV + FACE)

    accumulated = lax.map(one_domain, (blocks, next_blocks, next_maps, matrices, nodes))
    outgoing = accumulated[:, NODE_DEV:]
    returned = jnp.concatenate([jnp.zeros((1, FACE, OUT), jnp.float32), outgoing[:-1]], axis=0)

    def add_back(owned, where, values):
        return owned.at[where].add(values)

    applied = jax.vmap(add_back)(accumulated[:, :NODE_DEV], maps, returned)
    return applied.reshape(NODES, OUT)
```

```python
import functools

import jax
import jax.numpy as jnp
from jax import lax
from jax.experimental import pallas as pl
from jax.experimental.pallas import tpu as pltpu
from jax.sharding import PartitionSpec as P

MESH = pl.DeviceIdType.MESH
BF16, F32 = jnp.bfloat16, jnp.float32
XS, ZL, ZS, YS = 4, 16, 32, 4
DOMAIN = XS * ZL * 2
NT = (((1,), (1,)), ((), ()))
NN = (((1,), (0,)), ((), ()))
TN = (((0,), (0,)), ((), ()))


def dot(a, b, dims=NN):
    return lax.dot_general(a, b, dims, preferred_element_type=F32)


def two_words(value):
    high = value.astype(BF16)
    low = (value - high.astype(F32)).astype(BF16)
    return jnp.concatenate([high, low], axis=1)


def kernel(
    wf_hbm, rot_hbm, cell_hbm, nodes_ref, face_ref, out_ref,
    wf, held, cell, permuted, sent_y, came_y, sent_z, came_z, mine,
    corner_out, corner_in, face_out, face_in, back_out, back_in,
    load_sem, came, pair_came, express_sent, local_sent, x_sent, pair_sent,
    y_sent, y_came, z_sent, z_came, end_sent, end_came, token,
):
    d, b = lax.axis_index("domain"), lax.axis_index("band")
    x, z, core = d // 32, (d // 2) % ZL, d % 2
    y, zh = b // 2, b % 2
    q, r = z // 4, z % 4
    own, shared = out_ref.shape[0], face_ref.shape[1]
    cols = out_ref.shape[1]

    def along_z(step):
        far = (zh * ZL + z + step + ZS) % ZS
        return (x * 32 + (far % ZL) * 2 + core, y * 2 + far // ZL)

    def along_x(step):
        return (((x + step) % XS) * 32 + z * 2 + core, b)

    def along_y(step):
        return (d, ((y + step) % YS) * 2 + zh)

    def in_group(step):
        return (x * 32 + (q * 4 + (r + step) % 4) * 2 + core, b)

    pair = (x * 32 + z * 2 + (1 - core), b)
    across = (d, y * 2 + (1 - zh))

    def remote(source, target, send, recv, device):
        return pltpu.make_async_remote_copy(
            src_ref=source, dst_ref=target, send_sem=send, recv_sem=recv,
            device_id=device, device_id_type=MESH,
        )

    loads = [
        pltpu.make_async_copy(rot_hbm, held.at[d], load_sem.at[0]),
        pltpu.make_async_copy(wf_hbm, wf, load_sem.at[1]),
        pltpu.make_async_copy(cell_hbm, cell, load_sem.at[2]),
    ]
    for load in loads:
        load.start()

    barrier = pltpu.get_barrier_semaphore()
    greeted = [along_z(4), along_z(-4), pair]
    greeted += [f(i) for i in (1, 2, 3) for f in (in_group, along_x, along_y)]
    for device in greeted:
        pl.semaphore_signal(barrier, inc=1, device_id=device, device_id_type=MESH)
    pl.semaphore_wait(barrier, len(greeted))
    loads[0].wait()

    def slot(xx, zz):
        return held.at[(xx * ZL + zz) * 2 + core]

    def express(zz, up):
        way = 0 if up else 1
        return remote(
            slot(x, zz), slot(x, zz), express_sent.at[way, zz // 4],
            came.at[x * ZL + zz], along_z(4 if up else -4),
        )

    def local(zz, step):
        return remote(
            slot(x, zz), slot(x, zz), local_sent.at[step - 1, zz // 4],
            came.at[x * ZL + zz], in_group(step),
        )

    def over_x(zz, step):
        return remote(
            slot(x, zz), slot(x, zz), x_sent.at[step - 1, zz],
            came.at[x * ZL + zz], along_x(step),
        )

    def to_pair(xx, zz):
        index = xx * ZL + zz
        return remote(
            slot(xx, zz), slot(xx, zz), pair_sent.at[index],
            pair_came.at[index], pair,
        )

    def arrived(xx, zz):
        remote(
            slot(xx, zz), slot(xx, zz), pair_sent.at[xx * ZL + zz],
            came.at[xx * ZL + zz], pair,
        ).wait_recv()

    def spread(zz):
        for step in (1, 2, 3):
            over_x(zz, step).start()
        to_pair(x, zz).start()

    def from_group(qq):
        for step in (1, 2, 3):
            zz = qq * 4 + (r + step) % 4
            arrived(x, zz)
            spread(zz)

    def from_x(qq):
        for rr in range(4):
            for step in (1, 2, 3):
                xx = (x + step) % XS
                arrived(xx, qq * 4 + rr)
                to_pair(xx, qq * 4 + rr).start()

    pl.semaphore_signal(token, inc=1, device_id=along_z(4), device_id_type=MESH)

    @pl.when(q < 3)
    def _():
        express(z, True).start()

    @pl.when(q > 0)
    def _():
        express(z, False).start()

    for step in (1, 2, 3):
        local(z, step).start()
    spread(z)

    loads[2].wait()
    count = own + shared
    select = (
        lax.broadcasted_iota(jnp.int32, (count, count), 0) == nodes_ref[...]
    ).astype(F32).astype(BF16)
    rows = dot(select, cell[...]).astype(BF16)
    permuted[...] = dot(rows, select, NT).astype(BF16)

    @pl.when(d == 0)
    def _():
        corner_in[...] = jnp.zeros_like(corner_in)
        back_in[...] = jnp.zeros_like(back_in)

    @pl.when(d == DOMAIN - 1)
    def _():
        face_in[...] = jnp.zeros_like(face_in)

    from_group(q)

    def one_step(e, carry):
        pl.semaphore_wait(token, 1)
        pl.semaphore_signal(token, inc=1, device_id=along_z(4), device_id_type=MESH)
        low, high = q - e, q + e

        @pl.when(low >= 0)
        def _():
            zz = low * 4 + r
            arrived(x, zz)

            @pl.when(q < 3)
            def _():
                express(zz, True).start()

            for step in (1, 2, 3):
                local(zz, step).start()
            spread(zz)

        @pl.when(high <= 3)
        def _():
            zz = high * 4 + r
            arrived(x, zz)

            @pl.when(q > 0)
            def _():
                express(zz, False).start()

            for step in (1, 2, 3):
                local(zz, step).start()
            spread(zz)

        before_low, before_high = q - e + 1, q + e - 1

        @pl.when(before_low >= 0)
        def _():
            from_x(before_low)

        @pl.when(jnp.logical_and(before_high <= 3, e > 1))
        def _():
            from_x(before_high)

        @pl.when(low >= 0)
        def _():
            from_group(low)

        @pl.when(high <= 3)
        def _():
            from_group(high)

        return carry

    lax.fori_loop(1, 4, one_step, 0)
    pl.semaphore_wait(token, 1)

    @pl.when(q == 3)
    def _():
        from_x(0)

    @pl.when(q == 0)
    def _():
        from_x(3)

    loads[1].wait()

    def product(yy):
        for index in range(ZL):
            pltpu_wait = remote(
                held.at[0], held.at[0], pair_sent.at[0],
                pair_came.at[yy * ZL + index], pair,
            )
            pltpu_wait.wait_recv()
        block = held[pl.ds(yy * 32, 32)].astype(F32)
        block = block.reshape(2 * cols, block.shape[2]).astype(BF16)
        return dot(wf[...], block, NT)

    def y_copy(step, half):
        return remote(
            sent_y.at[step - 1, half], came_y.at[step - 1, half],
            y_sent.at[step - 1, half], y_came.at[step - 1, half], along_y(step),
        )

    for step in (2, 1, 3):
        part = product((y + step) % YS)
        low, high = part[:, :cols], part[:, cols:]
        sent_y[step - 1, 0] = jnp.where(zh == 0, high, low).astype(BF16)
        y_copy(step, 0).start()
        sent_y[step - 1, 1] = jnp.where(zh == 0, low, high).astype(BF16)
        y_copy(step, 1).start()
    part = product(y)
    low, high = part[:, :cols], part[:, cols:]
    other = jnp.where(zh == 0, high, low)
    mine[...] = jnp.where(zh == 0, low, high)

    for step in (1, 3, 2):
        y_copy(step, 0).wait_recv()
        other = other + came_y[step - 1, 0].astype(F32)
    sent_z[...] = other.astype(BF16)
    z_copy = remote(sent_z, came_z, z_sent, z_came, across)
    z_copy.start()

    after = (jnp.minimum(d + 1, DOMAIN - 1), b)
    before = (jnp.maximum(d - 1, 0), b)
    corner_copy = remote(corner_out, corner_in, end_sent.at[0], end_came.at[0], after)
    face_copy = remote(face_out, face_in, end_sent.at[1], end_came.at[1], before)
    back_copy = remote(back_out, back_in, end_sent.at[2], end_came.at[2], after)
    corner_out[...] = permuted[own:, own:]

    @pl.when(d < DOMAIN - 1)
    def _():
        corner_copy.start()

    total = mine[...]
    for step in (1, 3, 2):
        y_copy(step, 1).wait_recv()
        total = total + came_y[step - 1, 1].astype(F32)
    mine[...] = total
    pick = (
        lax.broadcasted_iota(jnp.int32, (own, shared), 0) == face_ref[...]
    ).astype(F32).astype(BF16)

    @pl.when(d > 0)
    def _():
        corner_copy.wait_recv()

    spread_corner = dot(pick, corner_in[...]).astype(BF16)

    z_copy.wait_recv()
    rotated = two_words(mine[...] + came_z[...].astype(F32))
    faces = dot(pick, rotated, TN).astype(BF16)
    face_out[...] = faces

    @pl.when(d > 0)
    def _():
        face_copy.start()

    back = dot(permuted[own:, :own], rotated)
    back_out[...] = two_words(back[:, :cols] + back[:, cols:])

    @pl.when(d < DOMAIN - 1)
    def _():
        back_copy.start()

    result = dot(permuted[:own, :own], rotated) + dot(spread_corner, faces)

    @pl.when(d < DOMAIN - 1)
    def _():
        face_copy.wait_recv()

    result = result + dot(permuted[:own, own:], face_in[...])

    @pl.when(d > 0)
    def _():
        back_copy.wait_recv()

    result = result + dot(pick, back_in[...])
    out_ref[...] = result[:, :cols] + result[:, cols:]

    for step in (1, 2, 3):
        for half in (0, 1):
            y_copy(step, half).wait_send()
    z_copy.wait_send()

    @pl.when(d < DOMAIN - 1)
    def _():
        corner_copy.wait_send()
        back_copy.wait_send()

    @pl.when(d > 0)
    def _():
        face_copy.wait_send()

    def sent_line(qq, carry):
        zz = qq * 4 + r

        @pl.when(jnp.logical_and(qq <= q, q < 3))
        def _():
            express(zz, True).wait_send()

        @pl.when(jnp.logical_and(qq >= q, q > 0))
        def _():
            express(zz, False).wait_send()

        for step in (1, 2, 3):
            local(zz, step).wait_send()
        return carry

    lax.fori_loop(0, 4, sent_line, 0)

    def sent_x(zz, carry):
        for step in (1, 2, 3):
            over_x(zz, step).wait_send()
        for xx in range(XS):
            to_pair(xx, zz).wait_send()
        return carry

    lax.fori_loop(0, ZL, sent_x, 0)


def local_step(wavefunctions, rotation, cell_matrices, cell_nodes, face_map):
    own, states = wavefunctions.shape
    shared = face_map.shape[0]
    count = own + shared
    cols = rotation.shape[1] * DOMAIN // 8
    dma = pltpu.SemaphoreType.DMA
    return pl.pallas_call(
        kernel,
        out_shape=jax.ShapeDtypeStruct((own, cols), F32),
        in_specs=[pl.BlockSpec(memory_space=pl.ANY)] * 3
        + [pl.BlockSpec(memory_space=pltpu.VMEM)] * 2,
        out_specs=pl.BlockSpec(memory_space=pltpu.VMEM),
        scratch_shapes=[
            pltpu.VMEM((own, states), BF16),
            pltpu.VMEM((DOMAIN, 8, states), BF16),
            pltpu.VMEM((count, count), BF16),
            pltpu.VMEM((count, count), BF16),
            pltpu.VMEM((3, 2, own, cols), BF16),
            pltpu.VMEM((3, 2, own, cols), BF16),
            pltpu.VMEM((own, cols), BF16),
            pltpu.VMEM((own, cols), BF16),
            pltpu.VMEM((own, cols), F32),
            pltpu.VMEM((shared, shared), BF16),
            pltpu.VMEM((shared, shared), BF16),
            pltpu.VMEM((shared, 2 * cols), BF16),
            pltpu.VMEM((shared, 2 * cols), BF16),
            pltpu.VMEM((shared, 2 * cols), BF16),
            pltpu.VMEM((shared, 2 * cols), BF16),
            dma((3,)),
            dma((XS * ZL,)),
            dma((XS * ZL,)),
            dma((2, 4)),
            dma((3, 4)),
            dma((3, ZL)),
            dma((XS * ZL,)),
            dma((3, 2)),
            dma((3, 2)),
            dma,
            dma,
            dma((3,)),
            dma((3,)),
            pltpu.SemaphoreType.REGULAR,
        ],
        compiler_params=pltpu.CompilerParams(collective_id=0, has_side_effects=True),
        name="rotate_and_apply",
    )(
        wavefunctions,
        rotation.T,
        cell_matrices.reshape(count, count),
        cell_nodes.reshape(1, count),
        face_map.reshape(1, shared),
    )


def solution(mesh):
    in_specs = (
        P("domain", "band"),
        P("band", "domain"),
        P("domain", None, None),
        P("domain", None),
        P("domain"),
    )
    out_specs = P("domain", "band")
    return jax.shard_map(
        local_step, mesh=mesh, in_specs=in_specs, out_specs=out_specs, check_vma=False
    )
```

```python
import functools

import jax
import jax.numpy as jnp
from jax import lax
from jax.experimental import pallas as pl
from jax.experimental.pallas import tpu as pltpu
from jax.sharding import PartitionSpec as P

MESH = pl.DeviceIdType.MESH
BF16, F32 = jnp.bfloat16, jnp.float32
XS, ZL, ZS, YS = 4, 16, 32, 4
DOMAIN = XS * ZL * 2
NT = (((1,), (1,)), ((), ()))
NN = (((1,), (0,)), ((), ()))
TN = (((0,), (0,)), ((), ()))


def dot(a, b, dims=NN):
    return lax.dot_general(a, b, dims, preferred_element_type=F32)


def two_words(value, axis):
    high = value.astype(BF16)
    low = (value - high.astype(F32)).astype(BF16)
    return jnp.concatenate([high, low], axis=axis)


def kernel(
    wf_hbm, rot_hbm, cell_hbm, nodes_ref, face_ref, out_ref,
    wf, held, cell, permuted, sent_y, came_y, kept, sent_z, came_z, mine,
    corner_out, corner_in, face_out, face_in, back_out, back_in,
    near_face_out, near_face_in, near_back_out, near_back_in,
    load_sem, came, pair_came, express_sent, local_sent, x_sent, pair_sent,
    y_sent, y_came, z_sent, z_came, end_sent, end_came, token,
):
    d, b = lax.axis_index("domain"), lax.axis_index("band")
    x, z, core = d // 32, (d // 2) % ZL, d % 2
    y, zh = b // 2, b % 2
    q, r = z // 4, z % 4
    own, shared = out_ref.shape[0], face_ref.shape[1]
    cols = out_ref.shape[1]
    some = cols // 2
    groups = (q, q + 1 - 2 * (q % 2), 2 - q // 2, 3 - 3 * (q // 2))
    ends_up = jnp.logical_and(d % 32 == 31, d < DOMAIN - 1)
    ends_down = jnp.logical_and(d % 32 == 0, d > 0)
    line_end = jnp.logical_or(ends_up, ends_down)

    def along_z(step):
        far = (zh * ZL + z + step + ZS) % ZS
        return (x * 32 + (far % ZL) * 2 + core, y * 2 + far // ZL)

    def along_x(step):
        return (((x + step) % XS) * 32 + z * 2 + core, b)

    def along_y(step):
        return (d, ((y + step) % YS) * 2 + zh)

    def in_group(step):
        return (x * 32 + (q * 4 + (r + step) % 4) * 2 + core, b)

    pair = (x * 32 + z * 2 + (1 - core), b)
    across = (d, y * 2 + (1 - zh))
    after = ((d + 1) % DOMAIN, b)
    before = ((d + DOMAIN - 1) % DOMAIN, b)
    near = ((d + DOMAIN + 2 * (d % 2) - 1) % DOMAIN, y * 2 + (1 - zh))

    def remote(source, target, send, recv, device):
        return pltpu.make_async_remote_copy(
            src_ref=source, dst_ref=target, send_sem=send, recv_sem=recv,
            device_id=device, device_id_type=MESH,
        )

    loads = [
        pltpu.make_async_copy(rot_hbm, held.at[d], load_sem.at[0]),
        pltpu.make_async_copy(wf_hbm, wf, load_sem.at[1]),
        pltpu.make_async_copy(cell_hbm, cell, load_sem.at[2]),
    ]
    for load in loads:
        load.start()

    barrier = pltpu.get_barrier_semaphore()
    greeted = [along_z(4), along_z(-4), pair]
    greeted += [f(i) for i in (1, 2, 3) for f in (in_group, along_x, along_y)]
    for device in greeted:
        pl.semaphore_signal(barrier, inc=1, device_id=device, device_id_type=MESH)

    @pl.when(line_end)
    def _():
        pl.semaphore_signal(barrier, inc=1, device_id=near, device_id_type=MESH)

    pl.semaphore_wait(barrier, len(greeted) + line_end.astype(jnp.int32))
    loads[0].wait()

    def slot(xx, zz):
        return held.at[(xx * ZL + zz) * 2 + core]

    def express(zz, up):
        way = 0 if up else 1
        return remote(
            slot(x, zz), slot(x, zz), express_sent.at[way, zz // 4],
            came.at[x * ZL + zz], along_z(4 if up else -4),
        )

    def local(zz, step):
        return remote(
            slot(x, zz), slot(x, zz), local_sent.at[step - 1, zz // 4],
            came.at[x * ZL + zz], in_group(step),
        )

    def over_x(zz, step):
        return remote(
            slot(x, zz), slot(x, zz), x_sent.at[step - 1, zz],
            came.at[x * ZL + zz], along_x(step),
        )

    def to_pair(xx, zz):
        index = xx * ZL + zz
        return remote(
            slot(xx, zz), slot(xx, zz), pair_sent.at[index],
            pair_came.at[index], pair,
        )

    def arrived(xx, zz):
        remote(
            slot(xx, zz), slot(xx, zz), pair_sent.at[xx * ZL + zz],
            came.at[xx * ZL + zz], pair,
        ).wait_recv()

    def spread(zz):
        for step in (1, 2, 3):
            over_x(zz, step).start()
        to_pair(x, zz).start()

    def from_group(qq):
        for step in (1, 2, 3):
            zz = qq * 4 + (r + step) % 4
            arrived(x, zz)
            spread(zz)

    def from_x(qq):
        for rr in range(4):
            for step in (1, 2, 3):
                xx = (x + step) % XS
                arrived(xx, qq * 4 + rr)
                to_pair(xx, qq * 4 + rr).start()

    pl.semaphore_signal(token, inc=1, device_id=along_z(4), device_id_type=MESH)

    @pl.when(q < 3)
    def _():
        express(z, True).start()

    @pl.when(q > 0)
    def _():
        express(z, False).start()

    for step in (1, 2, 3):
        local(z, step).start()
    spread(z)

    loads[2].wait()
    count = own + shared
    select = (
        lax.broadcasted_iota(jnp.int32, (count, count), 0) == nodes_ref[...]
    ).astype(F32).astype(BF16)
    rows = dot(select, cell[...]).astype(BF16)
    permuted[...] = dot(rows, select, NT).astype(BF16)

    pick = (
        lax.broadcasted_iota(jnp.int32, (own, shared), 0) == face_ref[...]
    ).astype(F32).astype(BF16)

    @pl.when(d == 0)
    def _():
        corner_in[...] = jnp.zeros_like(corner_in)
        back_in[...] = jnp.zeros_like(back_in)

    @pl.when(d == DOMAIN - 1)
    def _():
        face_in[...] = jnp.zeros_like(face_in)

    def pass_token():
        pl.semaphore_wait(token, 1)
        pl.semaphore_signal(token, inc=1, device_id=along_z(4), device_id_type=MESH)

    def from_express(qq):
        zz = qq * 4 + r
        arrived(x, zz)

        @pl.when(jnp.logical_and(qq < q, q < 3))
        def _():
            express(zz, True).start()

        @pl.when(jnp.logical_and(qq > q, q > 0))
        def _():
            express(zz, False).start()

        for step in (1, 2, 3):
            local(zz, step).start()
        spread(zz)

    def y_copy(n, step):
        return remote(
            sent_y.at[step - 1, n], came_y.at[step - 1, n],
            y_sent.at[step - 1, n], y_came.at[step - 1, n], along_y(step),
        )

    def z_copy(part):
        rows = pl.ds(pl.multiple_of(part * some, some), some)
        return remote(
            sent_z.at[rows], came_z.at[rows], z_sent.at[part], z_came.at[part], across
        )

    def product(n):
        qq = groups[n]
        for xx in range(XS):
            for rr in range(4):
                index = xx * ZL + qq * 4 + rr
                remote(
                    held.at[0], held.at[0], pair_sent.at[index],
                    pair_came.at[index], pair,
                ).wait_recv()
        pieces = [
            held[pl.ds((((y + step) % YS) * ZL + qq * 4) * 2, 8)].astype(F32)
            for step in range(YS)
        ]
        block = jnp.concatenate(pieces, axis=0)
        block = block.reshape(YS * some, block.shape[2]).astype(BF16)
        part = dot(block, wf[...], NT)
        for step in (2, 1, 3):
            sent_y[step - 1, n] = part[step * some:(step + 1) * some].astype(BF16)
            y_copy(n, step).start()
        kept[n] = part[:some]

    def summed(n):
        qq = groups[n]
        total = kept[n]
        for step in (1, 3, 2):
            y_copy(n, step).wait_recv()
            total = total + came_y[step - 1, n].astype(F32)
        part = qq % 2
        rows = pl.ds(pl.multiple_of(part * some, some), some)

        @pl.when(qq // 2 == zh)
        def _():
            mine[rows] = total

        @pl.when(qq // 2 != zh)
        def _():
            sent_z[rows] = total.astype(BF16)
            z_copy(part).start()

    from_group(groups[0])
    pass_token()
    from_express(groups[1])
    from_express(groups[2])
    pass_token()
    from_group(groups[1])
    from_x(groups[0])
    from_express(groups[3])
    pass_token()
    from_group(groups[2])
    loads[1].wait()
    product(0)
    from_x(groups[1])
    from_group(groups[3])
    pl.semaphore_wait(token, 1)
    product(1)
    summed(0)
    from_x(groups[2])
    product(2)
    summed(1)
    from_x(groups[3])
    product(3)
    summed(2)
    summed(3)

    corner_copy = remote(corner_out, corner_in, end_sent.at[0], end_came.at[0], after)
    face_copy = remote(face_out, face_in, end_sent.at[1], end_came.at[1], before)
    back_copy = remote(back_out, back_in, end_sent.at[2], end_came.at[2], after)
    near_face = remote(
        near_face_out, near_face_in, end_sent.at[3], end_came.at[3], near
    )
    near_back = remote(
        near_back_out, near_back_in, end_sent.at[4], end_came.at[4], near
    )

    @pl.when(ends_down)
    def _():
        face_out[...] = dot(two_words(mine[...], 0), pick).astype(BF16)
        face_copy.start()
        near_face_out[...] = dot(sent_z[...], pick).astype(BF16)
        near_face.start()

    def back_words(words):
        terms = dot(permuted[own:, :own], words, NT)
        if words.shape[0] > cols:
            terms = terms[:, :cols] + terms[:, cols:]
        return two_words(terms, 1)

    @pl.when(ends_up)
    def _():
        back_out[...] = back_words(two_words(mine[...], 0))
        back_copy.start()
        near_back_out[...] = back_words(sent_z[...])
        near_back.start()

    corner_out[...] = permuted[own:, own:]

    @pl.when(d < DOMAIN - 1)
    def _():
        corner_copy.start()

    @pl.when(d > 0)
    def _():
        corner_copy.wait_recv()

    spread_corner = dot(pick, corner_in[...]).astype(BF16)

    for part in (0, 1):
        z_copy(part).wait_recv()
    rotated = two_words(mine[...] + came_z[...].astype(F32), 0)
    faces = dot(rotated, pick).astype(BF16)

    sends_face = jnp.logical_and(d > 0, d % 32 != 0)
    sends_back = d % 32 != 31

    @pl.when(sends_face)
    def _():
        face_out[...] = faces
        face_copy.start()

    @pl.when(sends_back)
    def _():
        back_out[...] = back_words(rotated)
        back_copy.start()

    result = dot(permuted[:own, :own], rotated, NT) + dot(spread_corner, faces, NT)

    @pl.when(d < DOMAIN - 1)
    def _():
        face_copy.wait_recv()

    result = result + dot(permuted[:own, own:], face_in[...], NT)

    @pl.when(d > 0)
    def _():
        back_copy.wait_recv()

    result = result + dot(pick, back_in[...])
    out_ref[...] = result[:, :cols] + result[:, cols:]

    @pl.when(ends_up)
    def _():
        near_face.wait_recv()
        out_ref[...] += dot(permuted[:own, own:], near_face_in[...], NT)

    @pl.when(ends_down)
    def _():
        near_back.wait_recv()
        more = dot(pick, near_back_in[...])
        out_ref[...] += more[:, :cols] + more[:, cols:]

    for step in (1, 2, 3):
        for n in range(4):
            y_copy(n, step).wait_send()
    for part in (0, 1):
        z_copy(part).wait_send()

    @pl.when(d < DOMAIN - 1)
    def _():
        corner_copy.wait_send()
        back_copy.wait_send()

    @pl.when(d > 0)
    def _():
        face_copy.wait_send()

    @pl.when(ends_down)
    def _():
        near_face.wait_send()

    @pl.when(ends_up)
    def _():
        near_back.wait_send()

    def sent_line(qq, carry):
        zz = qq * 4 + r

        @pl.when(jnp.logical_and(qq <= q, q < 3))
        def _():
            express(zz, True).wait_send()

        @pl.when(jnp.logical_and(qq >= q, q > 0))
        def _():
            express(zz, False).wait_send()

        for step in (1, 2, 3):
            local(zz, step).wait_send()
        return carry

    lax.fori_loop(0, 4, sent_line, 0)

    def sent_x(zz, carry):
        for step in (1, 2, 3):
            over_x(zz, step).wait_send()
        for xx in range(XS):
            to_pair(xx, zz).wait_send()
        return carry

    lax.fori_loop(0, ZL, sent_x, 0)


def local_step(wavefunctions, rotation, cell_matrices, cell_nodes, face_map):
    own, states = wavefunctions.shape
    shared = face_map.shape[0]
    count = own + shared
    cols = rotation.shape[1] * DOMAIN // 8
    dma = pltpu.SemaphoreType.DMA
    return pl.pallas_call(
        kernel,
        out_shape=jax.ShapeDtypeStruct((own, cols), F32),
        in_specs=[pl.BlockSpec(memory_space=pl.ANY)] * 3
        + [pl.BlockSpec(memory_space=pltpu.VMEM)] * 2,
        out_specs=pl.BlockSpec(memory_space=pltpu.VMEM),
        scratch_shapes=[
            pltpu.VMEM((own, states), BF16),
            pltpu.VMEM((DOMAIN, 8, states), BF16),
            pltpu.VMEM((count, count), BF16),
            pltpu.VMEM((count, count), BF16),
            pltpu.VMEM((3, 4, cols // 2, own), BF16),
            pltpu.VMEM((3, 4, cols // 2, own), BF16),
            pltpu.VMEM((4, cols // 2, own), F32),
            pltpu.VMEM((cols, own), BF16),
            pltpu.VMEM((cols, own), BF16),
            pltpu.VMEM((cols, own), F32),
            pltpu.VMEM((shared, shared), BF16),
            pltpu.VMEM((shared, shared), BF16),
            pltpu.VMEM((2 * cols, shared), BF16),
            pltpu.VMEM((2 * cols, shared), BF16),
            pltpu.VMEM((shared, 2 * cols), BF16),
            pltpu.VMEM((shared, 2 * cols), BF16),
            pltpu.VMEM((cols, shared), BF16),
            pltpu.VMEM((cols, shared), BF16),
            pltpu.VMEM((shared, 2 * cols), BF16),
            pltpu.VMEM((shared, 2 * cols), BF16),
            dma((3,)),
            dma((XS * ZL,)),
            dma((XS * ZL,)),
            dma((2, 4)),
            dma((3, 4)),
            dma((3, ZL)),
            dma((XS * ZL,)),
            dma((3, 4)),
            dma((3, 4)),
            dma((2,)),
            dma((2,)),
            dma((5,)),
            dma((5,)),
            pltpu.SemaphoreType.REGULAR,
        ],
        compiler_params=pltpu.CompilerParams(collective_id=0, has_side_effects=True),
        name="rotate_and_apply",
    )(
        wavefunctions,
        rotation.T,
        cell_matrices.reshape(count, count),
        cell_nodes.reshape(1, count),
        face_map.reshape(1, shared),
    )


def solution(mesh):
    in_specs = (
        P("domain", "band"),
        P("band", "domain"),
        P("domain", None, None),
        P("domain", None),
        P("domain"),
    )
    out_specs = P("domain", "band")
    return jax.shard_map(
        local_step, mesh=mesh, in_specs=in_specs, out_specs=out_specs, check_vma=False
    )
```

```python
import functools

import jax
import jax.numpy as jnp
from jax import lax
from jax.experimental import pallas as pl
from jax.experimental.pallas import tpu as pltpu
from jax.sharding import PartitionSpec as P

MESH = pl.DeviceIdType.MESH
BF16, F32 = jnp.bfloat16, jnp.float32
XS, ZL, ZS, YS = 4, 16, 32, 4
DOMAIN = XS * ZL * 2
NT = (((1,), (1,)), ((), ()))
NN = (((1,), (0,)), ((), ()))
TN = (((0,), (0,)), ((), ()))


def dot(a, b, dims=NN):
    return lax.dot_general(a, b, dims, preferred_element_type=F32)


def two_words(value, axis):
    high = value.astype(BF16)
    low = (value - high.astype(F32)).astype(BF16)
    return jnp.concatenate([high, low], axis=axis)


def kernel(
    wf_hbm, rot_hbm, cell_hbm, nodes_ref, face_ref, out_ref,
    wf, held, cell, permuted, sent_y, came_y, kept, sent_z, came_z, mine,
    corner_out, corner_in, face_out, face_in, back_out, back_in,
    near_face_out, near_face_in, near_back_out, near_back_in,
    load_sem, came, x_came, pair_came, express_sent, local_sent, x_sent, pair_sent,
    y_sent, y_came, z_sent, z_came, end_sent, end_came, token,
):
    d, b = lax.axis_index("domain"), lax.axis_index("band")
    x, z, core = d // 32, (d // 2) % ZL, d % 2
    y, zh = b // 2, b % 2
    q, r = z // 4, z % 4
    own, shared = out_ref.shape[0], face_ref.shape[1]
    cols = out_ref.shape[1]
    some = cols // 2
    first = 1 + 2 * (r // 2)
    farthest = (first, 2, 4 - first)
    groups = (q, q + 1 - 2 * (q % 2), 2 - q // 2, 3 - 3 * (q // 2))
    ends_up = jnp.logical_and(d % 32 == 31, d < DOMAIN - 1)
    ends_down = jnp.logical_and(d % 32 == 0, d > 0)
    line_end = jnp.logical_or(ends_up, ends_down)

    def along_z(step):
        far = (zh * ZL + z + step + ZS) % ZS
        return (x * 32 + (far % ZL) * 2 + core, y * 2 + far // ZL)

    def along_x(step):
        return (((x + step) % XS) * 32 + z * 2 + core, b)

    def along_y(step):
        return (d, ((y + step) % YS) * 2 + zh)

    def in_group(step):
        return (x * 32 + (q * 4 + (r + step) % 4) * 2 + core, b)

    pair = (x * 32 + z * 2 + (1 - core), b)
    across = (d, y * 2 + (1 - zh))
    after = ((d + 1) % DOMAIN, b)
    before = ((d + DOMAIN - 1) % DOMAIN, b)
    near = ((d + DOMAIN + 2 * (d % 2) - 1) % DOMAIN, y * 2 + (1 - zh))

    def remote(source, target, send, recv, device):
        return pltpu.make_async_remote_copy(
            src_ref=source, dst_ref=target, send_sem=send, recv_sem=recv,
            device_id=device, device_id_type=MESH,
        )

    loads = [
        pltpu.make_async_copy(
            rot_hbm, held.at[core * (XS * ZL) + x * ZL + z], load_sem.at[0]
        ),
        pltpu.make_async_copy(wf_hbm, wf, load_sem.at[1]),
        pltpu.make_async_copy(cell_hbm, cell, load_sem.at[2]),
    ]
    for load in loads:
        load.start()

    barrier = pltpu.get_barrier_semaphore()
    greeted = [along_z(4), along_z(-4), pair]
    greeted += [f(i) for i in (1, 2, 3) for f in (in_group, along_x, along_y)]
    for device in greeted:
        pl.semaphore_signal(barrier, inc=1, device_id=device, device_id_type=MESH)

    @pl.when(line_end)
    def _():
        pl.semaphore_signal(barrier, inc=1, device_id=near, device_id_type=MESH)

    pl.semaphore_wait(barrier, len(greeted) + line_end.astype(jnp.int32))
    loads[0].wait()

    def slot(xx, zz):
        return held.at[core * (XS * ZL) + xx * ZL + zz]

    def four(xx, qq):
        return held.at[pl.ds(core * (XS * ZL) + xx * ZL + qq * 4, 4)]

    def express(zz, up):
        way = 0 if up else 1
        return remote(
            slot(x, zz), slot(x, zz), express_sent.at[way, zz // 4],
            came.at[zz], along_z(4 if up else -4),
        )

    def local(zz, step):
        return remote(
            slot(x, zz), slot(x, zz), local_sent.at[step - 1, zz // 4],
            came.at[zz], in_group(step),
        )

    def over_x(zz, step):
        return remote(
            slot(x, zz), slot(x, zz), x_sent.at[step - 1, zz],
            x_came.at[x, zz], along_x(step),
        )

    def to_pair(xx, qq):
        return remote(
            four(xx, qq), four(xx, qq), pair_sent.at[xx, qq],
            pair_came.at[xx, qq], pair,
        )

    def arrived(zz):
        remote(
            slot(x, zz), slot(x, zz), pair_sent.at[0, 0], came.at[zz], pair
        ).wait_recv()

    def spread(zz):
        for step in (2, 1, 3):
            over_x(zz, step).start()

    def from_group(qq):
        for step in (1, 2, 3):
            zz = qq * 4 + (r + step) % 4
            arrived(zz)
            spread(zz)
        to_pair(x, qq).start()

    def from_x(qq):
        for step in (1, 3, 2):
            xx = (x + step) % XS
            for rr in range(4):
                remote(
                    slot(xx, 0), slot(xx, 0), pair_sent.at[0, 0],
                    x_came.at[xx, qq * 4 + rr], pair,
                ).wait_recv()
            to_pair(xx, qq).start()

    pl.semaphore_signal(token, inc=1, device_id=along_z(4), device_id_type=MESH)

    @pl.when(q < 3)
    def _():
        express(z, True).start()

    @pl.when(q > 0)
    def _():
        express(z, False).start()

    for step in farthest:
        local(z, step).start()
    spread(z)

    @pl.when(d == 0)
    def _():
        corner_in[...] = jnp.zeros_like(corner_in)
        back_in[...] = jnp.zeros_like(back_in)

    @pl.when(d == DOMAIN - 1)
    def _():
        face_in[...] = jnp.zeros_like(face_in)

    def pass_token():
        pl.semaphore_wait(token, 1)
        pl.semaphore_signal(token, inc=1, device_id=along_z(4), device_id_type=MESH)

    def from_express(qq):
        zz = qq * 4 + r
        arrived(zz)

        @pl.when(jnp.logical_and(qq < q, q < 3))
        def _():
            express(zz, True).start()

        @pl.when(jnp.logical_and(qq > q, q > 0))
        def _():
            express(zz, False).start()

        for step in farthest:
            local(zz, step).start()
        spread(zz)

    def y_copy(n, step):
        return remote(
            sent_y.at[step - 1, n], came_y.at[step - 1, n],
            y_sent.at[step - 1, n], y_came.at[step - 1, n], along_y(step),
        )

    def z_copy(part):
        rows = pl.ds(pl.multiple_of(part * some, some), some)
        return remote(
            sent_z.at[rows], came_z.at[rows], z_sent.at[part], z_came.at[part], across
        )

    def product(n):
        qq = groups[n]
        for xx in range(XS):
            to_pair(xx, qq).wait_recv()
        pieces = [
            held[c * (XS * ZL) + ((y + step) % YS) * ZL + qq * 4 + rr].astype(F32)
            for step in range(YS)
            for rr in range(4)
            for c in (0, 1)
        ]
        block = jnp.concatenate(pieces, axis=0).astype(BF16)
        part = dot(block, wf[...], NT)
        for step in (2, 1, 3):
            sent_y[step - 1, n] = part[step * some:(step + 1) * some].astype(BF16)
            y_copy(n, step).start()
        kept[n] = part[:some]

    def summed(n):
        qq = groups[n]
        total = kept[n]
        for step in (1, 3, 2):
            y_copy(n, step).wait_recv()
            total = total + came_y[step - 1, n].astype(F32)
        part = qq % 2
        rows = pl.ds(pl.multiple_of(part * some, some), some)

        @pl.when(qq // 2 == zh)
        def _():
            mine[rows] = total

        @pl.when(qq // 2 != zh)
        def _():
            sent_z[rows] = total.astype(BF16)
            z_copy(part).start()

    from_group(groups[0])
    pass_token()
    from_express(groups[1])
    from_express(groups[2])
    pass_token()
    from_group(groups[1])
    from_x(groups[0])
    from_express(groups[3])
    pass_token()
    from_group(groups[2])
    loads[1].wait()
    product(0)
    from_x(groups[1])
    from_group(groups[3])
    pl.semaphore_wait(token, 1)
    product(1)
    summed(0)
    from_x(groups[2])
    product(2)
    summed(1)

    loads[2].wait()
    count = own + shared
    select = (
        lax.broadcasted_iota(jnp.int32, (count, count), 0) == nodes_ref[...]
    ).astype(F32).astype(BF16)
    rows = dot(select, cell[...]).astype(BF16)
    permuted[...] = dot(rows, select, NT).astype(BF16)

    pick = (
        lax.broadcasted_iota(jnp.int32, (own, shared), 0) == face_ref[...]
    ).astype(F32).astype(BF16)

    from_x(groups[3])
    product(3)
    summed(2)
    summed(3)

    corner_copy = remote(corner_out, corner_in, end_sent.at[0], end_came.at[0], after)
    face_copy = remote(face_out, face_in, end_sent.at[1], end_came.at[1], before)
    back_copy = remote(back_out, back_in, end_sent.at[2], end_came.at[2], after)
    near_face = remote(
        near_face_out, near_face_in, end_sent.at[3], end_came.at[3], near
    )
    near_back = remote(
        near_back_out, near_back_in, end_sent.at[4], end_came.at[4], near
    )

    @pl.when(ends_down)
    def _():
        face_out[...] = dot(two_words(mine[...], 0), pick).astype(BF16)
        face_copy.start()
        near_face_out[...] = dot(sent_z[...], pick).astype(BF16)
        near_face.start()

    def back_words(words):
        terms = dot(permuted[own:, :own], words, NT)
        if words.shape[0] > cols:
            terms = terms[:, :cols] + terms[:, cols:]
        return two_words(terms, 1)

    @pl.when(ends_up)
    def _():
        back_out[...] = back_words(two_words(mine[...], 0))
        back_copy.start()
        near_back_out[...] = back_words(sent_z[...])
        near_back.start()

    corner_out[...] = permuted[own:, own:]

    @pl.when(d < DOMAIN - 1)
    def _():
        corner_copy.start()

    @pl.when(d > 0)
    def _():
        corner_copy.wait_recv()

    spread_corner = dot(pick, corner_in[...]).astype(BF16)

    for part in (0, 1):
        z_copy(part).wait_recv()
    rotated = two_words(mine[...] + came_z[...].astype(F32), 0)
    faces = dot(rotated, pick).astype(BF16)

    sends_face = jnp.logical_and(d > 0, d % 32 != 0)
    sends_back = d % 32 != 31

    @pl.when(sends_face)
    def _():
        face_out[...] = faces
        face_copy.start()

    @pl.when(sends_back)
    def _():
        back_out[...] = back_words(rotated)
        back_copy.start()

    result = dot(permuted[:own, :own], rotated, NT) + dot(spread_corner, faces, NT)

    @pl.when(d < DOMAIN - 1)
    def _():
        face_copy.wait_recv()

    result = result + dot(permuted[:own, own:], face_in[...], NT)

    @pl.when(d > 0)
    def _():
        back_copy.wait_recv()

    result = result + dot(pick, back_in[...])
    out_ref[...] = result[:, :cols] + result[:, cols:]

    @pl.when(ends_up)
    def _():
        near_face.wait_recv()
        out_ref[...] += dot(permuted[:own, own:], near_face_in[...], NT)

    @pl.when(ends_down)
    def _():
        near_back.wait_recv()
        more = dot(pick, near_back_in[...])
        out_ref[...] += more[:, :cols] + more[:, cols:]

    for step in (1, 2, 3):
        for n in range(4):
            y_copy(n, step).wait_send()
    for part in (0, 1):
        z_copy(part).wait_send()

    @pl.when(d < DOMAIN - 1)
    def _():
        corner_copy.wait_send()
        back_copy.wait_send()

    @pl.when(d > 0)
    def _():
        face_copy.wait_send()

    @pl.when(ends_down)
    def _():
        near_face.wait_send()

    @pl.when(ends_up)
    def _():
        near_back.wait_send()

    def sent_line(qq, carry):
        zz = qq * 4 + r

        @pl.when(jnp.logical_and(qq <= q, q < 3))
        def _():
            express(zz, True).wait_send()

        @pl.when(jnp.logical_and(qq >= q, q > 0))
        def _():
            express(zz, False).wait_send()

        for step in (1, 2, 3):
            local(zz, step).wait_send()
        return carry

    lax.fori_loop(0, 4, sent_line, 0)

    def sent_x(zz, carry):
        for step in (1, 2, 3):
            over_x(zz, step).wait_send()
        return carry

    lax.fori_loop(0, ZL, sent_x, 0)
    for qq in range(4):
        for xx in range(XS):
            to_pair(xx, qq).wait_send()


def local_step(wavefunctions, rotation, cell_matrices, cell_nodes, face_map):
    own, states = wavefunctions.shape
    shared = face_map.shape[0]
    count = own + shared
    cols = rotation.shape[1] * DOMAIN // 8
    dma = pltpu.SemaphoreType.DMA
    return pl.pallas_call(
        kernel,
        out_shape=jax.ShapeDtypeStruct((own, cols), F32),
        in_specs=[pl.BlockSpec(memory_space=pl.ANY)] * 3
        + [pl.BlockSpec(memory_space=pltpu.VMEM)] * 2,
        out_specs=pl.BlockSpec(memory_space=pltpu.VMEM),
        scratch_shapes=[
            pltpu.VMEM((own, states), BF16),
            pltpu.VMEM((DOMAIN, 8, states), BF16),
            pltpu.VMEM((count, count), BF16),
            pltpu.VMEM((count, count), BF16),
            pltpu.VMEM((3, 4, cols // 2, own), BF16),
            pltpu.VMEM((3, 4, cols // 2, own), BF16),
            pltpu.VMEM((4, cols // 2, own), F32),
            pltpu.VMEM((cols, own), BF16),
            pltpu.VMEM((cols, own), BF16),
            pltpu.VMEM((cols, own), F32),
            pltpu.VMEM((shared, shared), BF16),
            pltpu.VMEM((shared, shared), BF16),
            pltpu.VMEM((2 * cols, shared), BF16),
            pltpu.VMEM((2 * cols, shared), BF16),
            pltpu.VMEM((shared, 2 * cols), BF16),
            pltpu.VMEM((shared, 2 * cols), BF16),
            pltpu.VMEM((cols, shared), BF16),
            pltpu.VMEM((cols, shared), BF16),
            pltpu.VMEM((shared, 2 * cols), BF16),
            pltpu.VMEM((shared, 2 * cols), BF16),
            dma((3,)),
            dma((ZL,)),
            dma((XS, ZL)),
            dma((XS, 4)),
            dma((2, 4)),
            dma((3, 4)),
            dma((3, ZL)),
            dma((XS, 4)),
            dma((3, 4)),
            dma((3, 4)),
            dma((2,)),
            dma((2,)),
            dma((5,)),
            dma((5,)),
            pltpu.SemaphoreType.REGULAR,
        ],
        compiler_params=pltpu.CompilerParams(collective_id=0, has_side_effects=True),
        name="rotate_and_apply",
    )(
        wavefunctions,
        rotation.T,
        cell_matrices.reshape(count, count),
        cell_nodes.reshape(1, count),
        face_map.reshape(1, shared),
    )


def solution(mesh):
    in_specs = (
        P("domain", "band"),
        P("band", "domain"),
        P("domain", None, None),
        P("domain", None),
        P("domain"),
    )
    out_specs = P("domain", "band")
    return jax.shard_map(
        local_step, mesh=mesh, in_specs=in_specs, out_specs=out_specs, check_vma=False
    )
```

```python
import functools

import jax
import jax.numpy as jnp
from jax import lax
from jax.experimental import pallas as pl
from jax.experimental.pallas import tpu as pltpu
from jax.sharding import PartitionSpec as P

MESH = pl.DeviceIdType.MESH
BF16, F32 = jnp.bfloat16, jnp.float32
XS, ZL, ZS, YS = 4, 16, 32, 4
DOMAIN = XS * ZL * 2
NT = (((1,), (1,)), ((), ()))
NN = (((1,), (0,)), ((), ()))
TN = (((0,), (0,)), ((), ()))


def dot(a, b, dims=NN):
    return lax.dot_general(a, b, dims, preferred_element_type=F32)


def two_words(value, axis):
    high = value.astype(BF16)
    low = (value - high.astype(F32)).astype(BF16)
    return jnp.concatenate([high, low], axis=axis)


def kernel(
    wf_hbm, rot_hbm, cell_hbm, nodes_ref, face_ref, out_ref,
    wf, held, cell, permuted, sent_y, came_y, kept, sent_z, came_z, mine,
    corner_out, corner_in, face_out, face_in, back_out, back_in,
    near_face_out, near_face_in, near_back_out, near_back_in,
    load_sem, came, x_came, pair_came, express_sent, local_sent, x_sent, pair_sent,
    y_sent, y_came, z_sent, z_came, end_sent, end_came, token,
):
    d, b = lax.axis_index("domain"), lax.axis_index("band")
    x, z, core = d // 32, (d // 2) % ZL, d % 2
    y, zh = b // 2, b % 2
    q, r = z // 4, z % 4
    own, shared = out_ref.shape[0], face_ref.shape[1]
    cols = out_ref.shape[1]
    some = cols // 2
    first = 1 + 2 * (r // 2)
    farthest = (first, 2, 4 - first)
    groups = (q, q + 1 - 2 * (q % 2), 2 - q // 2, 3 - 3 * (q // 2))
    ends_up = jnp.logical_and(d % 32 == 31, d < DOMAIN - 1)
    ends_down = jnp.logical_and(d % 32 == 0, d > 0)
    line_end = jnp.logical_or(ends_up, ends_down)

    def along_z(step):
        far = (zh * ZL + z + step + ZS) % ZS
        return (x * 32 + (far % ZL) * 2 + core, y * 2 + far // ZL)

    def along_x(step):
        return (((x + step) % XS) * 32 + z * 2 + core, b)

    def along_y(step):
        return (d, ((y + step) % YS) * 2 + zh)

    def in_group(step):
        return (x * 32 + (q * 4 + (r + step) % 4) * 2 + core, b)

    pair = (x * 32 + z * 2 + (1 - core), b)
    across = (d, y * 2 + (1 - zh))
    after = ((d + 1) % DOMAIN, b)
    before = ((d + DOMAIN - 1) % DOMAIN, b)
    near = ((d + DOMAIN + 2 * (d % 2) - 1) % DOMAIN, y * 2 + (1 - zh))

    def remote(source, target, send, recv, device):
        return pltpu.make_async_remote_copy(
            src_ref=source, dst_ref=target, send_sem=send, recv_sem=recv,
            device_id=device, device_id_type=MESH,
        )

    loads = [
        pltpu.make_async_copy(
            rot_hbm, held.at[core * (XS * ZL) + x * ZL + z], load_sem.at[0]
        ),
        pltpu.make_async_copy(wf_hbm, wf, load_sem.at[1]),
        pltpu.make_async_copy(cell_hbm, cell, load_sem.at[2]),
    ]
    for load in loads:
        load.start()

    barrier = pltpu.get_barrier_semaphore()
    greeted = [along_z(4), along_z(-4), pair]
    greeted += [f(i) for i in (1, 2, 3) for f in (in_group, along_x, along_y)]
    for device in greeted:
        pl.semaphore_signal(barrier, inc=1, device_id=device, device_id_type=MESH)

    @pl.when(line_end)
    def _():
        pl.semaphore_signal(barrier, inc=1, device_id=near, device_id_type=MESH)

    pl.semaphore_wait(barrier, len(greeted) + line_end.astype(jnp.int32))
    loads[0].wait()

    def slot(xx, zz):
        return held.at[core * (XS * ZL) + xx * ZL + zz]

    def four(xx, qq):
        return held.at[pl.ds(core * (XS * ZL) + xx * ZL + qq * 4, 4)]

    def express(zz, up):
        way = 0 if up else 1
        return remote(
            slot(x, zz), slot(x, zz), express_sent.at[way, zz // 4],
            came.at[zz], along_z(4 if up else -4),
        )

    def local(zz, step):
        return remote(
            slot(x, zz), slot(x, zz), local_sent.at[step - 1, zz // 4],
            came.at[zz], in_group(step),
        )

    def over_x(zz, step):
        return remote(
            slot(x, zz), slot(x, zz), x_sent.at[step - 1, zz],
            x_came.at[x, zz], along_x(step),
        )

    def to_pair(xx, qq):
        return remote(
            four(xx, qq), four(xx, qq), pair_sent.at[xx, qq],
            pair_came.at[xx, qq], pair,
        )

    def arrived(zz):
        remote(
            slot(x, zz), slot(x, zz), pair_sent.at[0, 0], came.at[zz], pair
        ).wait_recv()

    def spread(zz):
        for step in (2, 1, 3):
            over_x(zz, step).start()

    def from_group(qq):
        for step in (1, 2, 3):
            zz = qq * 4 + (r + step) % 4
            arrived(zz)
            spread(zz)
        to_pair(x, qq).start()

    def from_x(qq):
        for step in (1, 3, 2):
            xx = (x + step) % XS
            for rr in range(4):
                remote(
                    slot(xx, 0), slot(xx, 0), pair_sent.at[0, 0],
                    x_came.at[xx, qq * 4 + rr], pair,
                ).wait_recv()
            to_pair(xx, qq).start()

    pl.semaphore_signal(token, inc=1, device_id=along_z(4), device_id_type=MESH)

    @pl.when(q < 3)
    def _():
        express(z, True).start()

    @pl.when(q > 0)
    def _():
        express(z, False).start()

    spread(z)
    for step in farthest:
        local(z, step).start()

    @pl.when(d == 0)
    def _():
        corner_in[...] = jnp.zeros_like(corner_in)
        back_in[...] = jnp.zeros_like(back_in)

    @pl.when(d == DOMAIN - 1)
    def _():
        face_in[...] = jnp.zeros_like(face_in)

    def pass_token():
        pl.semaphore_wait(token, 1)
        pl.semaphore_signal(token, inc=1, device_id=along_z(4), device_id_type=MESH)

    def from_express(qq):
        zz = qq * 4 + r
        arrived(zz)

        @pl.when(jnp.logical_and(qq < q, q < 3))
        def _():
            express(zz, True).start()

        @pl.when(jnp.logical_and(qq > q, q > 0))
        def _():
            express(zz, False).start()

        spread(zz)
        for step in farthest:
            local(zz, step).start()

    def y_copy(n, step):
        return remote(
            sent_y.at[step - 1, n], came_y.at[step - 1, n],
            y_sent.at[step - 1, n], y_came.at[step - 1, n], along_y(step),
        )

    def z_copy(part):
        rows = pl.ds(pl.multiple_of(part * some, some), some)
        return remote(
            sent_z.at[rows], came_z.at[rows], z_sent.at[part], z_came.at[part], across
        )

    def product(n):
        qq = groups[n]
        for xx in range(XS):
            to_pair(xx, qq).wait_recv()
        pieces = [
            held[c * (XS * ZL) + ((y + step) % YS) * ZL + qq * 4 + rr].astype(F32)
            for step in range(YS)
            for rr in range(4)
            for c in (0, 1)
        ]
        block = jnp.concatenate(pieces, axis=0).astype(BF16)
        part = dot(block, wf[...], NT)
        for step in (1, 3, 2):
            sent_y[step - 1, n] = part[step * some:(step + 1) * some].astype(BF16)
            y_copy(n, step).start()
        kept[n] = part[:some]

    def summed(n):
        qq = groups[n]
        total = kept[n]
        for step in (1, 3, 2):
            y_copy(n, step).wait_recv()
            total = total + came_y[step - 1, n].astype(F32)
        part = qq % 2
        rows = pl.ds(pl.multiple_of(part * some, some), some)

        @pl.when(qq // 2 == zh)
        def _():
            mine[rows] = total

        @pl.when(qq // 2 != zh)
        def _():
            sent_z[rows] = total.astype(BF16)
            z_copy(part).start()

    from_group(groups[0])
    pass_token()
    from_express(groups[1])
    from_express(groups[2])
    pass_token()
    from_group(groups[1])
    from_x(groups[0])
    from_express(groups[3])
    pass_token()
    from_group(groups[2])
    loads[1].wait()
    product(0)
    from_x(groups[1])
    from_group(groups[3])
    pl.semaphore_wait(token, 1)
    product(1)
    summed(0)
    from_x(groups[2])
    product(2)
    summed(1)

    loads[2].wait()
    count = own + shared
    select = (
        lax.broadcasted_iota(jnp.int32, (count, count), 0) == nodes_ref[...]
    ).astype(F32).astype(BF16)
    rows = dot(select, cell[...]).astype(BF16)
    permuted[...] = dot(rows, select, NT).astype(BF16)

    pick = (
        lax.broadcasted_iota(jnp.int32, (own, shared), 0) == face_ref[...]
    ).astype(F32).astype(BF16)

    from_x(groups[3])
    product(3)
    summed(2)
    summed(3)

    corner_copy = remote(corner_out, corner_in, end_sent.at[0], end_came.at[0], after)
    face_copy = remote(face_out, face_in, end_sent.at[1], end_came.at[1], before)
    back_copy = remote(back_out, back_in, end_sent.at[2], end_came.at[2], after)
    near_face = remote(
        near_face_out, near_face_in, end_sent.at[3], end_came.at[3], near
    )
    near_back = remote(
        near_back_out, near_back_in, end_sent.at[4], end_came.at[4], near
    )

    @pl.when(ends_down)
    def _():
        face_out[...] = dot(two_words(mine[...], 0), pick).astype(BF16)
        face_copy.start()
        near_face_out[...] = dot(sent_z[...], pick).astype(BF16)
        near_face.start()

    def back_words(words):
        terms = dot(permuted[own:, :own], words, NT)
        if words.shape[0] > cols:
            terms = terms[:, :cols] + terms[:, cols:]
        return two_words(terms, 1)

    @pl.when(ends_up)
    def _():
        back_out[...] = back_words(two_words(mine[...], 0))
        back_copy.start()
        near_back_out[...] = back_words(sent_z[...])
        near_back.start()

    corner_out[...] = permuted[own:, own:]

    @pl.when(d < DOMAIN - 1)
    def _():
        corner_copy.start()

    @pl.when(d > 0)
    def _():
        corner_copy.wait_recv()

    spread_corner = dot(pick, corner_in[...]).astype(BF16)

    for part in (0, 1):
        z_copy(part).wait_recv()
    rotated = two_words(mine[...] + came_z[...].astype(F32), 0)
    faces = dot(rotated, pick).astype(BF16)

    sends_face = jnp.logical_and(d > 0, d % 32 != 0)
    sends_back = d % 32 != 31

    @pl.when(sends_face)
    def _():
        face_out[...] = faces
        face_copy.start()

    @pl.when(sends_back)
    def _():
        back_out[...] = back_words(rotated)
        back_copy.start()

    result = dot(permuted[:own, :own], rotated, NT) + dot(spread_corner, faces, NT)

    @pl.when(d < DOMAIN - 1)
    def _():
        face_copy.wait_recv()

    result = result + dot(permuted[:own, own:], face_in[...], NT)

    @pl.when(d > 0)
    def _():
        back_copy.wait_recv()

    result = result + dot(pick, back_in[...])
    out_ref[...] = result[:, :cols] + result[:, cols:]

    @pl.when(ends_up)
    def _():
        near_face.wait_recv()
        out_ref[...] += dot(permuted[:own, own:], near_face_in[...], NT)

    @pl.when(ends_down)
    def _():
        near_back.wait_recv()
        more = dot(pick, near_back_in[...])
        out_ref[...] += more[:, :cols] + more[:, cols:]

    for step in (1, 2, 3):
        for n in range(4):
            y_copy(n, step).wait_send()
    for part in (0, 1):
        z_copy(part).wait_send()

    @pl.when(d < DOMAIN - 1)
    def _():
        corner_copy.wait_send()
        back_copy.wait_send()

    @pl.when(d > 0)
    def _():
        face_copy.wait_send()

    @pl.when(ends_down)
    def _():
        near_face.wait_send()

    @pl.when(ends_up)
    def _():
        near_back.wait_send()

    def sent_line(qq, carry):
        zz = qq * 4 + r

        @pl.when(jnp.logical_and(qq <= q, q < 3))
        def _():
            express(zz, True).wait_send()

        @pl.when(jnp.logical_and(qq >= q, q > 0))
        def _():
            express(zz, False).wait_send()

        for step in (1, 2, 3):
            local(zz, step).wait_send()
        return carry

    lax.fori_loop(0, 4, sent_line, 0)

    def sent_x(zz, carry):
        for step in (1, 2, 3):
            over_x(zz, step).wait_send()
        return carry

    lax.fori_loop(0, ZL, sent_x, 0)
    for qq in range(4):
        for xx in range(XS):
            to_pair(xx, qq).wait_send()


def local_step(wavefunctions, rotation, cell_matrices, cell_nodes, face_map):
    own, states = wavefunctions.shape
    shared = face_map.shape[0]
    count = own + shared
    cols = rotation.shape[1] * DOMAIN // 8
    dma = pltpu.SemaphoreType.DMA
    return pl.pallas_call(
        kernel,
        out_shape=jax.ShapeDtypeStruct((own, cols), F32),
        in_specs=[pl.BlockSpec(memory_space=pl.ANY)] * 3
        + [pl.BlockSpec(memory_space=pltpu.VMEM)] * 2,
        out_specs=pl.BlockSpec(memory_space=pltpu.VMEM),
        scratch_shapes=[
            pltpu.VMEM((own, states), BF16),
            pltpu.VMEM((DOMAIN, 8, states), BF16),
            pltpu.VMEM((count, count), BF16),
            pltpu.VMEM((count, count), BF16),
            pltpu.VMEM((3, 4, cols // 2, own), BF16),
            pltpu.VMEM((3, 4, cols // 2, own), BF16),
            pltpu.VMEM((4, cols // 2, own), F32),
            pltpu.VMEM((cols, own), BF16),
            pltpu.VMEM((cols, own), BF16),
            pltpu.VMEM((cols, own), F32),
            pltpu.VMEM((shared, shared), BF16),
            pltpu.VMEM((shared, shared), BF16),
            pltpu.VMEM((2 * cols, shared), BF16),
            pltpu.VMEM((2 * cols, shared), BF16),
            pltpu.VMEM((shared, 2 * cols), BF16),
            pltpu.VMEM((shared, 2 * cols), BF16),
            pltpu.VMEM((cols, shared), BF16),
            pltpu.VMEM((cols, shared), BF16),
            pltpu.VMEM((shared, 2 * cols), BF16),
            pltpu.VMEM((shared, 2 * cols), BF16),
            dma((3,)),
            dma((ZL,)),
            dma((XS, ZL)),
            dma((XS, 4)),
            dma((2, 4)),
            dma((3, 4)),
            dma((3, ZL)),
            dma((XS, 4)),
            dma((3, 4)),
            dma((3, 4)),
            dma((2,)),
            dma((2,)),
            dma((5,)),
            dma((5,)),
            pltpu.SemaphoreType.REGULAR,
        ],
        compiler_params=pltpu.CompilerParams(collective_id=0, has_side_effects=True),
        name="rotate_and_apply",
    )(
        wavefunctions,
        rotation.T,
        cell_matrices.reshape(count, count),
        cell_nodes.reshape(1, count),
        face_map.reshape(1, shared),
    )


def solution(mesh):
    in_specs = (
        P("domain", "band"),
        P("band", "domain"),
        P("domain", None, None),
        P("domain", None),
        P("domain"),
    )
    out_specs = P("domain", "band")
    return jax.shard_map(
        local_step, mesh=mesh, in_specs=in_specs, out_specs=out_specs, check_vma=False
    )
```

```python
import functools

import jax
import jax.numpy as jnp
from jax import lax
from jax.experimental import pallas as pl
from jax.experimental.pallas import tpu as pltpu
from jax.sharding import PartitionSpec as P

MESH = pl.DeviceIdType.MESH
BF16, F32 = jnp.bfloat16, jnp.float32
XS, ZL, ZS, YS = 4, 16, 32, 4
DOMAIN = XS * ZL * 2
NT = (((1,), (1,)), ((), ()))
NN = (((1,), (0,)), ((), ()))
TN = (((0,), (0,)), ((), ()))


def dot(a, b, dims=NN):
    return lax.dot_general(a, b, dims, preferred_element_type=F32)


def two_words(value, axis):
    high = value.astype(BF16)
    low = (value - high.astype(F32)).astype(BF16)
    return jnp.concatenate([high, low], axis=axis)


def kernel(
    wf_hbm, rot_hbm, cell_hbm, nodes_ref, face_ref, out_ref,
    wf, held, cell, permuted, sent_y, came_y, kept, sent_z, came_z, mine,
    corner_out, corner_in, face_out, face_in, back_out, back_in,
    near_face_out, near_face_in, near_back_out, near_back_in,
    load_sem, came, x_came, pair_came, express_sent, local_sent, x_sent, pair_sent,
    y_sent, y_came, z_sent, z_came, end_sent, end_came, token,
):
    d, b = lax.axis_index("domain"), lax.axis_index("band")
    x, z, core = d // 32, (d // 2) % ZL, d % 2
    y, zh = b // 2, b % 2
    q, r = z // 4, z % 4
    own, shared = out_ref.shape[0], face_ref.shape[1]
    cols = out_ref.shape[1]
    some = cols // 2
    first = 1 + 2 * (r // 2)
    farthest = (first, 2, 4 - first)
    groups = (q, q + 1 - 2 * (q % 2), 2 - q // 2, 3 - 3 * (q // 2))
    ends_up = jnp.logical_and(d % 32 == 31, d < DOMAIN - 1)
    ends_down = jnp.logical_and(d % 32 == 0, d > 0)
    line_end = jnp.logical_or(ends_up, ends_down)

    def along_z(step):
        far = (zh * ZL + z + step + ZS) % ZS
        return (x * 32 + (far % ZL) * 2 + core, y * 2 + far // ZL)

    def along_x(step):
        return (((x + step) % XS) * 32 + z * 2 + core, b)

    def along_y(step):
        return (d, ((y + step) % YS) * 2 + zh)

    def in_group(step):
        return (x * 32 + (q * 4 + (r + step) % 4) * 2 + core, b)

    pair = (x * 32 + z * 2 + (1 - core), b)
    across = (d, y * 2 + (1 - zh))
    after = ((d + 1) % DOMAIN, b)
    before = ((d + DOMAIN - 1) % DOMAIN, b)
    near = ((d + DOMAIN + 2 * (d % 2) - 1) % DOMAIN, y * 2 + (1 - zh))

    def remote(source, target, send, recv, device):
        return pltpu.make_async_remote_copy(
            src_ref=source, dst_ref=target, send_sem=send, recv_sem=recv,
            device_id=device, device_id_type=MESH,
        )

    loads = [
        pltpu.make_async_copy(
            rot_hbm, held.at[core * (XS * ZL) + x * ZL + z], load_sem.at[0]
        ),
        pltpu.make_async_copy(wf_hbm, wf, load_sem.at[1]),
        pltpu.make_async_copy(cell_hbm, cell, load_sem.at[2]),
    ]
    for load in loads:
        load.start()

    barrier = pltpu.get_barrier_semaphore()
    greeted = [along_z(4), along_z(-4), pair]
    greeted += [f(i) for i in (1, 2, 3) for f in (in_group, along_x, along_y)]
    for device in greeted:
        pl.semaphore_signal(barrier, inc=1, device_id=device, device_id_type=MESH)

    @pl.when(line_end)
    def _():
        pl.semaphore_signal(barrier, inc=1, device_id=near, device_id_type=MESH)

    pl.semaphore_wait(barrier, len(greeted) + line_end.astype(jnp.int32))
    loads[0].wait()

    def slot(xx, zz):
        return held.at[core * (XS * ZL) + xx * ZL + zz]

    def four(xx, qq):
        return held.at[pl.ds(core * (XS * ZL) + xx * ZL + qq * 4, 4)]

    def express(zz, up):
        way = 0 if up else 1
        return remote(
            slot(x, zz), slot(x, zz), express_sent.at[way, zz // 4],
            came.at[zz], along_z(4 if up else -4),
        )

    def local(zz, step):
        return remote(
            slot(x, zz), slot(x, zz), local_sent.at[step - 1, zz // 4],
            came.at[zz], in_group(step),
        )

    def over_x(zz, step):
        return remote(
            slot(x, zz), slot(x, zz), x_sent.at[step - 1, zz],
            x_came.at[x, zz], along_x(step),
        )

    def to_pair(xx, qq):
        return remote(
            four(xx, qq), four(xx, qq), pair_sent.at[xx, qq],
            pair_came.at[xx, qq], pair,
        )

    def arrived(zz):
        remote(
            slot(x, zz), slot(x, zz), pair_sent.at[0, 0], came.at[zz], pair
        ).wait_recv()

    def spread(zz):
        for step in (2, 1, 3):
            over_x(zz, step).start()

    def from_group(qq):
        for step in (1, 2, 3):
            zz = qq * 4 + (r + step) % 4
            arrived(zz)
            spread(zz)
        to_pair(x, qq).start()

    def from_x(qq):
        for step in (1, 3, 2):
            xx = (x + step) % XS
            for rr in range(4):
                remote(
                    slot(xx, 0), slot(xx, 0), pair_sent.at[0, 0],
                    x_came.at[xx, qq * 4 + rr], pair,
                ).wait_recv()
            to_pair(xx, qq).start()

    pl.semaphore_signal(token, inc=1, device_id=along_z(4), device_id_type=MESH)

    @pl.when(q < 3)
    def _():
        express(z, True).start()

    @pl.when(q > 0)
    def _():
        express(z, False).start()

    spread(z)
    for step in farthest:
        local(z, step).start()

    @pl.when(d == 0)
    def _():
        corner_in[...] = jnp.zeros_like(corner_in)
        back_in[...] = jnp.zeros_like(back_in)

    @pl.when(d == DOMAIN - 1)
    def _():
        face_in[...] = jnp.zeros_like(face_in)

    def pass_token():
        pl.semaphore_wait(token, 1)
        pl.semaphore_signal(token, inc=1, device_id=along_z(4), device_id_type=MESH)

    def from_express(qq):
        zz = qq * 4 + r
        arrived(zz)

        @pl.when(jnp.logical_and(qq < q, q < 3))
        def _():
            express(zz, True).start()

        @pl.when(jnp.logical_and(qq > q, q > 0))
        def _():
            express(zz, False).start()

        spread(zz)
        for step in farthest:
            local(zz, step).start()

    def y_copy(n, step):
        return remote(
            sent_y.at[step - 1, n], came_y.at[step - 1, n],
            y_sent.at[step - 1, n], y_came.at[step - 1, n], along_y(step),
        )

    def z_copy(part):
        rows = pl.ds(pl.multiple_of(part * some, some), some)
        return remote(
            sent_z.at[rows], came_z.at[rows], z_sent.at[part], z_came.at[part], across
        )

    def product(n):
        qq = groups[n]
        for xx in range(XS):
            to_pair(xx, qq).wait_recv()
        pieces = [
            held[c * (XS * ZL) + ((y + step) % YS) * ZL + qq * 4 + rr].astype(F32)
            for step in range(YS)
            for rr in range(4)
            for c in (0, 1)
        ]
        block = jnp.concatenate(pieces, axis=0).astype(BF16)
        part = dot(block, wf[...], NT)
        for step in (1, 3, 2):
            sent_y[step - 1, n] = part[step * some:(step + 1) * some].astype(BF16)
            y_copy(n, step).start()
        kept[n] = part[:some]

    def summed(n):
        qq = groups[n]
        total = kept[n]
        for step in (1, 3, 2):
            y_copy(n, step).wait_recv()
            total = total + came_y[step - 1, n].astype(F32)
        part = qq % 2
        rows = pl.ds(pl.multiple_of(part * some, some), some)

        @pl.when(qq // 2 == zh)
        def _():
            mine[rows] = total

        @pl.when(qq // 2 != zh)
        def _():
            sent_z[rows] = total.astype(BF16)
            z_copy(part).start()

    from_group(groups[0])
    pass_token()
    from_express(groups[1])
    from_express(groups[2])
    pass_token()
    from_group(groups[1])
    from_x(groups[0])
    from_express(groups[3])
    pass_token()
    from_group(groups[2])
    loads[1].wait()
    product(0)
    from_x(groups[1])
    from_group(groups[3])
    pl.semaphore_wait(token, 1)
    product(1)
    summed(0)
    from_x(groups[2])
    product(2)
    summed(1)
    from_x(groups[3])
    product(3)
    summed(2)
    summed(3)

    loads[2].wait()
    count = own + shared
    select = (
        lax.broadcasted_iota(jnp.int32, (count, count), 0) == nodes_ref[...]
    ).astype(F32).astype(BF16)
    rows = dot(select, cell[...]).astype(BF16)
    permuted[...] = dot(rows, select, NT).astype(BF16)

    pick = (
        lax.broadcasted_iota(jnp.int32, (own, shared), 0) == face_ref[...]
    ).astype(F32).astype(BF16)

    corner_copy = remote(corner_out, corner_in, end_sent.at[0], end_came.at[0], after)
    face_copy = remote(face_out, face_in, end_sent.at[1], end_came.at[1], before)
    back_copy = remote(back_out, back_in, end_sent.at[2], end_came.at[2], after)
    near_face = remote(
        near_face_out, near_face_in, end_sent.at[3], end_came.at[3], near
    )
    near_back = remote(
        near_back_out, near_back_in, end_sent.at[4], end_came.at[4], near
    )

    @pl.when(ends_down)
    def _():
        face_out[...] = dot(two_words(mine[...], 0), pick).astype(BF16)
        face_copy.start()
        near_face_out[...] = dot(sent_z[...], pick).astype(BF16)
        near_face.start()

    def back_words(words):
        terms = dot(permuted[own:, :own], words, NT)
        if words.shape[0] > cols:
            terms = terms[:, :cols] + terms[:, cols:]
        return two_words(terms, 1)

    @pl.when(ends_up)
    def _():
        back_out[...] = back_words(two_words(mine[...], 0))
        back_copy.start()
        near_back_out[...] = back_words(sent_z[...])
        near_back.start()

    corner_out[...] = permuted[own:, own:]

    @pl.when(d < DOMAIN - 1)
    def _():
        corner_copy.start()

    @pl.when(d > 0)
    def _():
        corner_copy.wait_recv()

    spread_corner = dot(pick, corner_in[...]).astype(BF16)

    for part in (0, 1):
        z_copy(part).wait_recv()
    rotated = two_words(mine[...] + came_z[...].astype(F32), 0)
    faces = dot(rotated, pick).astype(BF16)

    sends_face = jnp.logical_and(d > 0, d % 32 != 0)
    sends_back = d % 32 != 31

    @pl.when(sends_face)
    def _():
        face_out[...] = faces
        face_copy.start()

    @pl.when(sends_back)
    def _():
        back_out[...] = back_words(rotated)
        back_copy.start()

    result = dot(permuted[:own, :own], rotated, NT) + dot(spread_corner, faces, NT)

    @pl.when(d < DOMAIN - 1)
    def _():
        face_copy.wait_recv()

    result = result + dot(permuted[:own, own:], face_in[...], NT)

    @pl.when(d > 0)
    def _():
        back_copy.wait_recv()

    result = result + dot(pick, back_in[...])
    out_ref[...] = result[:, :cols] + result[:, cols:]

    @pl.when(ends_up)
    def _():
        near_face.wait_recv()
        out_ref[...] += dot(permuted[:own, own:], near_face_in[...], NT)

    @pl.when(ends_down)
    def _():
        near_back.wait_recv()
        more = dot(pick, near_back_in[...])
        out_ref[...] += more[:, :cols] + more[:, cols:]

    for step in (1, 2, 3):
        for n in range(4):
            y_copy(n, step).wait_send()
    for part in (0, 1):
        z_copy(part).wait_send()

    @pl.when(d < DOMAIN - 1)
    def _():
        corner_copy.wait_send()
        back_copy.wait_send()

    @pl.when(d > 0)
    def _():
        face_copy.wait_send()

    @pl.when(ends_down)
    def _():
        near_face.wait_send()

    @pl.when(ends_up)
    def _():
        near_back.wait_send()

    def sent_line(qq, carry):
        zz = qq * 4 + r

        @pl.when(jnp.logical_and(qq <= q, q < 3))
        def _():
            express(zz, True).wait_send()

        @pl.when(jnp.logical_and(qq >= q, q > 0))
        def _():
            express(zz, False).wait_send()

        for step in (1, 2, 3):
            local(zz, step).wait_send()
        return carry

    lax.fori_loop(0, 4, sent_line, 0)

    def sent_x(zz, carry):
        for step in (1, 2, 3):
            over_x(zz, step).wait_send()
        return carry

    lax.fori_loop(0, ZL, sent_x, 0)
    for qq in range(4):
        for xx in range(XS):
            to_pair(xx, qq).wait_send()


def local_step(wavefunctions, rotation, cell_matrices, cell_nodes, face_map):
    own, states = wavefunctions.shape
    shared = face_map.shape[0]
    count = own + shared
    cols = rotation.shape[1] * DOMAIN // 8
    dma = pltpu.SemaphoreType.DMA
    return pl.pallas_call(
        kernel,
        out_shape=jax.ShapeDtypeStruct((own, cols), F32),
        in_specs=[pl.BlockSpec(memory_space=pl.ANY)] * 3
        + [pl.BlockSpec(memory_space=pltpu.VMEM)] * 2,
        out_specs=pl.BlockSpec(memory_space=pltpu.VMEM),
        scratch_shapes=[
            pltpu.VMEM((own, states), BF16),
            pltpu.VMEM((DOMAIN, 8, states), BF16),
            pltpu.VMEM((count, count), BF16),
            pltpu.VMEM((count, count), BF16),
            pltpu.VMEM((3, 4, cols // 2, own), BF16),
            pltpu.VMEM((3, 4, cols // 2, own), BF16),
            pltpu.VMEM((4, cols // 2, own), F32),
            pltpu.VMEM((cols, own), BF16),
            pltpu.VMEM((cols, own), BF16),
            pltpu.VMEM((cols, own), F32),
            pltpu.VMEM((shared, shared), BF16),
            pltpu.VMEM((shared, shared), BF16),
            pltpu.VMEM((2 * cols, shared), BF16),
            pltpu.VMEM((2 * cols, shared), BF16),
            pltpu.VMEM((shared, 2 * cols), BF16),
            pltpu.VMEM((shared, 2 * cols), BF16),
            pltpu.VMEM((cols, shared), BF16),
            pltpu.VMEM((cols, shared), BF16),
            pltpu.VMEM((shared, 2 * cols), BF16),
            pltpu.VMEM((shared, 2 * cols), BF16),
            dma((3,)),
            dma((ZL,)),
            dma((XS, ZL)),
            dma((XS, 4)),
            dma((2, 4)),
            dma((3, 4)),
            dma((3, ZL)),
            dma((XS, 4)),
            dma((3, 4)),
            dma((3, 4)),
            dma((2,)),
            dma((2,)),
            dma((5,)),
            dma((5,)),
            pltpu.SemaphoreType.REGULAR,
        ],
        compiler_params=pltpu.CompilerParams(collective_id=0, has_side_effects=True),
        name="rotate_and_apply",
    )(
        wavefunctions,
        rotation.T,
        cell_matrices.reshape(count, count),
        cell_nodes.reshape(1, count),
        face_map.reshape(1, shared),
    )


def solution(mesh):
    in_specs = (
        P("domain", "band"),
        P("band", "domain"),
        P("domain", None, None),
        P("domain", None),
        P("domain"),
    )
    out_specs = P("domain", "band")
    return jax.shard_map(
        local_step, mesh=mesh, in_specs=in_specs, out_specs=out_specs, check_vma=False
    )
```
